32 devices in a mesh: groups: 2 (over x), cell: 16 (over z, y, core).
Axes of the slice: x: 2, y: 2, z: 4, core: 2. Of those that a mesh axis runs over, the one named last changes fastest.
Arguments:
- frames: bfloat16 [4096, 8, 512], P(('groups', 'cell')), parts along dimension 0
- norm_time: float32 [512], replicated, may hold values from 0.1 to 1.9
- t_wq: bfloat16 [512, 512], replicated
- t_wkv: bfloat16 [512, 1024], replicated
- t_wo: bfloat16 [512, 512], replicated, may hold values from -0.25 to 0.25
- norm_space: float32 [512], replicated, may hold values from 0.1 to 1.9
- s_wq: bfloat16 [512, 512], replicated
- s_wkv: bfloat16 [512, 1024], replicated
- s_wo: bfloat16 [512, 512], replicated, may hold values from -0.25 to 0.25
- norm_mlp: float32 [512], replicated, may hold values from 0.1 to 1.9
- w_gate: bfloat16 [512, 2048], replicated, may hold values from -0.25 to 0.25
- w_up: bfloat16 [512, 2048], replicated, may hold values from -0.25 to 0.25
- w_down: bfloat16 [2048, 512], replicated, may hold values from -0.125 to 0.125
- nbr_blocks: int32 [32, 3], P(('groups', 'cell')), parts along dimension 0, may hold values from 0 to 15, as said below
- nbr_count: int32 [32], P(('groups', 'cell')), parts along dimension 0, may hold values from 1 to 3, as said below
Outputs:
- forecast_rows: bfloat16 [4096, 8, 512], P(('groups', 'cell')), parts along dimension 0
The draws below stay inside these ranges and needn't reach their ends.
There are 2 independent parts, one for each index of `groups`. The reference program is written for one: setup_inputs(seed, part) draws one part's arguments, and reference() takes and returns one part's arrays. A program takes and returns all parts, laid end to end along the dimension named above; an argument that names none is the same for every part. Nothing has to cross between parts.
Inputs may be any that keep to these rules, and one draw needn't show every extreme that they name: `nbr_blocks`: row b lists distinct blocks b + o modulo 16 with 1 <= |o| <= 2; only the first nbr_count[b] entries of a row are used, the others are such blocks too. Block 0 lists block 15 and block 1 lists block 0, each as its first entry. `nbr_count`: some block uses all 3 entries and some block uses one.
All inputs are finite; a program needn't handle non-finite values.
Results may differ from the reference program's by a relative error of at most 0.018.
Values may be sent and summed in bfloat16 or wider, within the bound.
No kernel may reach another device: no remote copies, remote signals or barrier semaphores. Data moves between devices by JAX's collectives and lax.ppermute only.
A program may use at most 128 MiB of HBM per device.

```python
import math
import jax
import jax.numpy as jnp
from jax import lax

D = 512
HEADS = 8
HEAD_DIM = 64
FF = 2048
TIME = 8
BLOCK = 128
NBR_MAX = 3
CELLS = 2048
BLOCKS = 16
REACH = 2
N_CELL = 16


def draw_frames(key, part):
    shape = (CELLS, TIME, D)
    return jnp.clip(jax.random.normal(key, shape, jnp.float32), -6.0, 6.0).astype(jnp.bfloat16)


def query_key(key, salt, which):
    base = jax.random.fold_in(key, salt)
    kq, kk = jax.random.split(base, 2)
    w_query = jax.random.normal(kq, (D, D), jnp.float32) / math.sqrt(D)
    w_pair = jax.random.normal(kk, (D, 2 * D), jnp.float32) / math.sqrt(D)
    if which == 0:
        return w_query
    return w_pair


def draw_t_wq(key, part):
    return query_key(key, 3, 0).astype(jnp.bfloat16)


def draw_t_wkv(key, part):
    return query_key(key, 3, 1).astype(jnp.bfloat16)


def draw_s_wq(key, part):
    return query_key(key, 5, 0).astype(jnp.bfloat16)


def draw_s_wkv(key, part):
    return query_key(key, 5, 1).astype(jnp.bfloat16)


def neighbour_lists(key):
    base = jax.random.fold_in(key, 11)
    k1, k2, k3 = jax.random.split(base, 3)
    counts = jax.random.randint(k1, (BLOCKS,), 1, NBR_MAX + 1)
    spot = jax.random.randint(k2, (), 0, BLOCKS)
    counts = counts.at[spot].set(NBR_MAX)
    counts = counts.at[(spot + 1) % BLOCKS].set(1)
    offsets = jnp.concatenate([-jnp.arange(1, REACH + 1), jnp.arange(1, REACH + 1)]).astype(jnp.int32)
    scores = jax.random.randint(k3, (BLOCKS, 2 * REACH), 0, 2 ** 20) * (2 * REACH) + jnp.arange(2 * REACH)
    scores = scores.at[0:2, 0].set(-1)
    order = jnp.argsort(scores, axis=1)[:, :NBR_MAX]
    listed = (jnp.arange(BLOCKS)[:, None] + offsets[order]) % BLOCKS
    return (listed.astype(jnp.int32), counts.astype(jnp.int32))


def draw_nbr_blocks(key, part):
    return neighbour_lists(key)[0]


def draw_nbr_count(key, part):
    return neighbour_lists(key)[1]


def noise(rng, shape, scale, most, held_as=jnp.bfloat16):
    values = jax.random.normal(rng, shape, jnp.float32) * scale
    return jnp.minimum(jnp.maximum(values, -most), most).astype(held_as)


def setup_inputs(seed: int = 0, part: int = 0) -> dict:
    key_list = jax.random.split(jax.random.key(seed), 16)
    part_keys = jax.random.split(jax.random.fold_in(key_list[15], part), 16)
    frames = draw_frames(jax.random.fold_in(jax.random.fold_in(key_list[15], part), 71), part)
    norm_time = jnp.clip(1.0 + 0.18 * jax.random.normal(key_list[1], (D,), jnp.float32), 0.1, 1.9)
    t_wq = draw_t_wq(jax.random.fold_in(key_list[15], 71), part)
    t_wkv = draw_t_wkv(jax.random.fold_in(key_list[15], 71), part)
    t_wo = noise(key_list[4], (D, D), D ** -0.5, 0.25)
    norm_space = jnp.clip(1.0 + 0.18 * jax.random.normal(key_list[5], (D,), jnp.float32), 0.1, 1.9)
    s_wq = draw_s_wq(jax.random.fold_in(key_list[15], 71), part)
    s_wkv = draw_s_wkv(jax.random.fold_in(key_list[15], 71), part)
    s_wo = noise(key_list[8], (D, D), D ** -0.5, 0.25)
    norm_mlp = jnp.clip(1.0 + 0.18 * jax.random.normal(key_list[9], (D,), jnp.float32), 0.1, 1.9)
    w_gate = noise(key_list[10], (D, FF), D ** -0.5, 0.25)
    w_up = noise(key_list[11], (D, FF), D ** -0.5, 0.25)
    w_down = noise(key_list[12], (FF, D), FF ** -0.5, 0.125)
    nbr_blocks = draw_nbr_blocks(jax.random.fold_in(jax.random.fold_in(key_list[15], part), 71), part)
    nbr_count = draw_nbr_count(jax.random.fold_in(jax.random.fold_in(key_list[15], part), 71), part)
    return {"frames": frames, "norm_time": norm_time, "t_wq": t_wq, "t_wkv": t_wkv, "t_wo": t_wo, "norm_space": norm_space, "s_wq": s_wq, "s_wkv": s_wkv, "s_wo": s_wo, "norm_mlp": norm_mlp, "w_gate": w_gate, "w_up": w_up, "w_down": w_down, "nbr_blocks": nbr_blocks, "nbr_count": nbr_count}


EPS = 1e-05

def norm_rows(rows, gain):
    wide = rows.astype(jnp.float32)
    scaled = wide * lax.rsqrt(lax.optimization_barrier(jnp.mean(wide * wide, axis=-1, keepdims=True)) + EPS)
    return (scaled * gain).astype(jnp.bfloat16)

def project_wide(rows, weight):
    lead = rows.shape[:-1]
    flat = rows.reshape(-1, rows.shape[-1])
    return jnp.dot(flat, weight, preferred_element_type=jnp.float32).reshape(lead + (weight.shape[1],))

def temporal_mix(normed, t_wq, t_wkv, t_wo):
    cells = normed.shape[0]
    query = project_wide(normed, t_wq).astype(jnp.bfloat16).reshape(cells, TIME, HEADS, HEAD_DIM)
    pairs = project_wide(normed, t_wkv).astype(jnp.bfloat16)
    keys = pairs[..., :D].reshape(cells, TIME, HEADS, HEAD_DIM)
    values = pairs[..., D:].reshape(cells, TIME, HEADS, HEAD_DIM)
    scores = jnp.einsum('cthe,cuhe->chtu', query.astype(jnp.float32), keys.astype(jnp.float32)) / math.sqrt(HEAD_DIM)
    causal = jnp.arange(TIME)[:, None] >= jnp.arange(TIME)[None, :]
    scores = jnp.where(causal, scores, -1e+30)
    probs = jax.nn.softmax(scores, axis=-1).astype(jnp.bfloat16)
    context = jnp.einsum('chtu,cuhe->cthe', probs.astype(jnp.float32), values.astype(jnp.float32)).astype(jnp.bfloat16)
    return project_wide(context.reshape(cells, TIME, D), t_wo)

def reference(frames, norm_time, t_wq, t_wkv, t_wo, norm_space, s_wq, s_wkv, s_wo, norm_mlp, w_gate, w_up, w_down, nbr_blocks, nbr_count):
    cells_all = frames.shape[0]
    normed = norm_rows(frames, norm_time)
    mixed = (frames.astype(jnp.float32) + temporal_mix(normed, t_wq, t_wkv, t_wo)).astype(jnp.bfloat16)
    per_dev = cells_all // N_CELL
    slice_cells = per_dev // N_CELL
    spaced_rows = mixed.reshape(N_CELL, N_CELL, slice_cells, TIME, D).transpose(1, 0, 2, 3, 4).reshape(cells_all, TIME, D)
    spaced_norm = norm_rows(spaced_rows, norm_space)
    query = project_wide(spaced_norm, s_wq).astype(jnp.bfloat16)
    pairs = project_wide(spaced_norm, s_wkv).astype(jnp.bfloat16)
    blocks_all = cells_all // BLOCK
    query_blocks = query.reshape(blocks_all, BLOCK, TIME, HEADS, HEAD_DIM)
    key_blocks = pairs[..., :D].reshape(blocks_all, BLOCK, TIME, HEADS, HEAD_DIM)
    value_blocks = pairs[..., D:].reshape(blocks_all, BLOCK, TIME, HEADS, HEAD_DIM)

    def one_block(item):
        block_id, own_query, listed, count = item
        picks = jnp.concatenate([block_id[None], listed]).astype(jnp.int32)
        live = jnp.concatenate([jnp.ones((1,), dtype=bool), jnp.arange(NBR_MAX) < count])
        chosen_keys = key_blocks[picks].astype(jnp.float32)
        chosen_values = value_blocks[picks].astype(jnp.float32)
        scores = jnp.einsum('qthe,skthe->thqsk', own_query.astype(jnp.float32), chosen_keys) / math.sqrt(HEAD_DIM)
        scores = jnp.where(live[None, None, None, :, None], scores, -1e+30)
        flat = scores.reshape(TIME, HEADS, BLOCK, -1)
        probs = jax.nn.softmax(flat, axis=-1).astype(jnp.bfloat16).reshape(scores.shape)
        return jnp.einsum('thqsk,skthe->qthe', probs.astype(jnp.float32), chosen_values).astype(jnp.bfloat16)
    context = lax.map(one_block, (jnp.arange(blocks_all).astype(jnp.int32), query_blocks, nbr_blocks, nbr_count))
    context = context.reshape(cells_all, TIME, D)
    after_space = (spaced_rows.astype(jnp.float32) + project_wide(context, s_wo)).astype(jnp.bfloat16)
    mlp_in = norm_rows(after_space, norm_mlp)
    hidden = (jax.nn.silu(project_wide(mlp_in, w_gate)) * project_wide(mlp_in, w_up)).astype(jnp.bfloat16)
    return (after_space.astype(jnp.float32) + project_wide(hidden, w_down)).astype(jnp.bfloat16)
```

```python
import functools

import jax
import jax.numpy as jnp
from jax import lax
from jax.experimental import pallas as pl
from jax.experimental.pallas import tpu as pltpu
from jax.sharding import PartitionSpec as P

HEADS = 8
HEAD_DIM = 64
EPS = 1e-05
NEG = -1e30
PIECES = 4
MIB = 1 << 20


f32 = jnp.float32
bf16 = jnp.bfloat16


def normed(wide, gain):
    scale = lax.rsqrt(jnp.mean(wide * wide, axis=-1, keepdims=True) + EPS)
    return (wide * scale * gain).astype(bf16)


def mm(a, b):
    return jnp.dot(a, b, preferred_element_type=f32)


def mm_t(a, b):
    return lax.dot_general(a, b, (((1,), (1,)), ((), ())), preferred_element_type=f32)


def spread_heads(rows, group):
    if group == 1:
        return rows
    head = lax.broadcasted_iota(jnp.int32, rows.shape, 1) // HEAD_DIM
    zero = jnp.zeros_like(rows)
    return jnp.concatenate([jnp.where(head == h, rows, zero) for h in range(group)], axis=0)


def attend(query, key, value, group, mask):
    rows = query.shape[0]
    lanes = query.shape[1]
    scores = mm_t(spread_heads(query, group), key)
    if mask is not None:
        scores = jnp.where(mask, scores, NEG)
    top = jnp.max(scores, axis=-1, keepdims=True)
    probs = jnp.exp(scores - top).astype(bf16)
    ones = jnp.ones(value.shape, bf16)
    both = mm(probs, jnp.concatenate([value, ones], axis=1))
    context = both[:, :lanes] / both[:, lanes:]
    if group == 1:
        return context
    head = lax.broadcasted_iota(jnp.int32, (rows, lanes), 1) // HEAD_DIM
    merged = context[:rows]
    for h in range(1, group):
        merged = jnp.where(head == h, context[h * rows : (h + 1) * rows], merged)
    return merged


def temporal_kernel(axis, share, blocks, nbr_ref, count_ref, frames_ref, gain_ref, wq_ref, wkv_ref,
                    wo_ref, *rest):
    outs, rows_ref = rest[:-1], rest[-1]
    step = pl.program_id(0)
    cells, steps, width = frames_ref.shape
    rows = cells * steps
    me = lax.axis_index(axis)
    slot = me // share
    wide = frames_ref[...].astype(f32).reshape(rows, width)
    x = normed(wide, gain_ref[...])
    query = (mm(x, wq_ref[...]) * (HEAD_DIM**-0.5)).astype(bf16)
    pairs = mm(x, wkv_ref[...]).astype(bf16)
    tile = 128
    r = lax.broadcasted_iota(jnp.int32, (2 * tile, tile), 0) % tile
    c = lax.broadcasted_iota(jnp.int32, (2 * tile, tile), 1)
    mask = (r // steps == c // steps) & (c <= r)
    parts = []
    for base in range(0, rows, tile):
        here = slice(base, base + tile)
        parts.append(jnp.concatenate([
            attend(query[here, at : at + 128], pairs[here, at : at + 128],
                   pairs[here, width + at : width + at + 128], 2, mask).astype(bf16)
            for at in range(0, width, 128)
        ], axis=1))
    context = jnp.concatenate(parts, axis=0)
    mixed = wide + mm(context, wo_ref[...])
    for at in range(0, width, 128):
        rows_ref[at // 128] = mixed[:, at : at + 128]
    for peer, out_ref in enumerate(outs):
        when = slot ^ peer
        here = pl.ds(pl.multiple_of(step * cells, cells), cells)
        for at in range(0, width, 128):
            out_ref[here, at : at + 128] = rows_ref[
                at // 128, pl.ds(when, cells, stride=steps), :
            ].astype(bf16)

    @pl.when(step == 0)
    def _():
        extra = 8
        total = outs[0].shape[0] - extra
        lane = lax.broadcasted_iota(jnp.int32, (extra, width), 1)
        note = jnp.where(lane == 0, count_ref[0], 0)
        for i in range(nbr_ref.shape[0]):
            hop = (nbr_ref[i] - me + blocks + blocks // 2) % blocks - blocks // 2
            note = jnp.where(lane == i + 1, hop, note)
        note = note.astype(f32).astype(bf16)
        for out_ref in outs:
            out_ref[pl.ds(total, extra), :] = note


def temporal(frames, gain, wq, wkv, wo, nbr, count, axis, share, blocks):
    cells, steps, width = frames.shape
    grid = 4
    part = cells // grid
    whole = lambda *shape: pl.BlockSpec(shape, lambda i, *_: (0,) * len(shape))
    message = cells + 8
    return pl.pallas_call(
        functools.partial(temporal_kernel, axis, share, blocks),
        grid_spec=pltpu.PrefetchScalarGridSpec(
            num_scalar_prefetch=2,
            grid=(grid,),
            in_specs=[
                pl.BlockSpec((part, steps, width), lambda i, *_: (i, 0, 0)),
                whole(1, width),
                whole(*wq.shape),
                whole(*wkv.shape),
                whole(*wo.shape),
            ],
            out_specs=[whole(message, width)] * steps,
            scratch_shapes=[pltpu.VMEM((width // 128, part * steps, 128), f32)],
        ),
        out_shape=[jax.ShapeDtypeStruct((message, width), bf16)] * steps,
        compiler_params=pltpu.CompilerParams(vmem_limit_bytes=24 * MIB),
        cost_estimate=pl.CostEstimate(
            flops=2 * cells * steps * width * width * 4, bytes_accessed=6 * MIB, transcendentals=0
        ),
        name="temporal",
    )(nbr.reshape(-1), count, frames, gain.reshape(1, width), wq, wkv, wo)


def project_kernel(axis, share, steps, in_pieces, *refs):
    total = share * steps if in_pieces else 2
    ins, rest = refs[:total], refs[total:]
    gain_ref, wq_ref, wk_ref, wv_ref, q_ref, k_ref, v_ref, x_ref, notes_ref = rest[:9]
    me = lax.axis_index(axis)
    slot, member = me // share, me % share
    blocks, block, width = rest[9].shape if in_pieces else (share * steps, *rest[9].shape)
    chunk = block // blocks
    if in_pieces:
        spaced_ref = rest[9]
        for d in range(share):
            for r in range(steps):
                source = (slot ^ r) * share + (member + share - d) % share
                piece = ins[d * steps + r]
                spaced_ref[:, pl.ds(pl.multiple_of(source * chunk, chunk), chunk), :] = (
                    piece[:block, :].astype(f32).reshape(blocks, chunk, width)
                )
                notes_ref[pl.ds(source, 1), :] = (
                    piece[block : block + 8, :128].astype(f32)[:1].astype(jnp.int32)
                )
        rows_of = lambda b: spaced_ref[b]
    else:
        notes_ref[...] = ins[1][...]
        rows_of = lambda b: ins[0][pl.ds(pl.multiple_of(b * block, block), block), :].astype(f32)

    @pl.loop(0, blocks // 2)
    def _(i):
        wide = jnp.concatenate([rows_of(2 * i), rows_of(2 * i + 1)], axis=0)
        x = normed(wide, gain_ref[...])
        here = pl.ds(pl.multiple_of(i * 2 * block, 2 * block), 2 * block)
        q_ref[here, :] = (mm(x, wq_ref[...]) * (HEAD_DIM**-0.5)).astype(bf16)
        k_ref[here, :] = mm(x, wk_ref[...]).astype(bf16)
        v_ref[here, :] = mm(x, wv_ref[...]).astype(bf16)

    for r in range(steps):
        x_ref[r * block : (r + 1) * block, :] = rows_of((slot ^ r) * share + member).astype(bf16)


def project(pieces, gain, wq, wkv, axis, share, member):
    steps = len(pieces[0])
    blocks = share * steps
    message, width = pieces[0][0].shape
    block = message - 8
    mine = width // share
    chunk = block // blocks
    in_pieces = chunk % 8 == 0
    if in_pieces:
        ins = [p for ps in pieces for p in ps]
        scratch = [pltpu.VMEM((blocks, block, width), f32)]
    else:
        me = lax.axis_index(axis)
        slot = me // share
        order = jnp.array([0])
        source = jnp.arange(blocks)
        d = (me % share - source % share) % share
        order = d * steps + (source // share ^ slot)
        stacked = jnp.take(jnp.stack([p for ps in pieces for p in ps]), order, axis=0)
        rows = stacked[:, :block].reshape(blocks, blocks, chunk, width).transpose(1, 0, 2, 3)
        ins = [rows.reshape(blocks * block, width), stacked[:, block, :128].astype(jnp.int32)]
        scratch = [pltpu.VMEM((block, width), f32)]
    whole = lambda shape: pl.BlockSpec(shape, lambda i, *_: (0,) * len(shape))
    if mine % 128 == 0:
        cols = lambda at: pl.BlockSpec((width, mine), lambda i, m: (0, at * share + m[0]))
        weights, w_specs = [wq, wkv, wkv], [cols(0), cols(0), cols(1)]
    else:
        take = lambda w, at: lax.dynamic_slice_in_dim(w, at * width + member[0] * mine, mine, axis=1)
        weights = [take(wq, 0), take(wkv, 0), take(wkv, 1)]
        w_specs = [whole((width, mine))] * 3
    out_shapes = [((blocks * block, mine), bf16)] * 3 + [((steps * block, width), bf16), ((blocks, 128), jnp.int32)]
    body = functools.partial(project_kernel, axis, share, steps, in_pieces)
    return pl.pallas_call(
        lambda m_ref, *refs: body(*refs),
        grid_spec=pltpu.PrefetchScalarGridSpec(
            num_scalar_prefetch=1,
            grid=(1,),
            in_specs=[whole(a.shape) for a in ins] + [whole((1, width))] + w_specs,
            out_specs=[whole(s) for s, _ in out_shapes],
            scratch_shapes=scratch,
        ),
        out_shape=[jax.ShapeDtypeStruct(s, t) for s, t in out_shapes],
        compiler_params=pltpu.CompilerParams(vmem_limit_bytes=(24 if in_pieces else 48) * MIB),
        cost_estimate=pl.CostEstimate(
            flops=2 * blocks * block * width * mine * 3, bytes_accessed=6 * MIB, transcendentals=0
        ),
        name="project",
    )(member, *ins, gain.reshape(1, width), *weights)


def spatial_kernel(axis, share, peers, listed, notes_ref, q_ref, k_ref, v_ref, *rest):
    outs, work_ref = rest[:-1], rest[-1]
    block = work_ref.shape[1]
    width = work_ref.shape[2]
    blocks = q_ref.shape[0] // block
    me = lax.axis_index(axis)
    slot, member = me // share, me % share
    group = min(2, width // HEAD_DIM)
    lanes = group * HEAD_DIM
    count = len(peers)
    at = lambda b: pl.ds(pl.multiple_of(b * block, block), block)

    @pl.loop(0, count * share)
    def _(i):
        r = peers[0] + i // share
        b = (slot ^ r) * share + (member + i % share) % share
        used = notes_ref[b, 0]
        place = (i % share) * count + i // share
        for n in range(1, listed + 1):
            @pl.when(used == n)
            def _():
                keys = [at(b)]
                for k in range(n):
                    keys.append(at((b + notes_ref[b, 1 + k] + blocks) % blocks))
                for lane in range(0, width, lanes):
                    cols = slice(lane, lane + lanes)
                    key = jnp.concatenate([k_ref[k, cols] for k in keys], axis=0)
                    value = jnp.concatenate([v_ref[k, cols] for k in keys], axis=0)
                    context = attend(q_ref[at(b), cols], key, value, group, None)
                    work_ref[place, :, cols] = context.astype(bf16)

    for d, out_ref in enumerate(outs):
        for k in range(count):
            out_ref[k * block : (k + 1) * block, :] = work_ref[d * count + k]


def spatial(notes, q, k, v, block, peers, listed, axis, share):
    mine = q.shape[1]
    whole = lambda shape: pl.BlockSpec(shape, lambda i, *_: (0,) * len(shape))
    out = (len(peers) * block, mine)
    return pl.pallas_call(
        functools.partial(spatial_kernel, axis, share, peers, listed),
        grid_spec=pltpu.PrefetchScalarGridSpec(
            num_scalar_prefetch=1,
            grid=(1,),
            in_specs=[whole(q.shape)] * 3,
            out_specs=[whole(out)] * share,
            scratch_shapes=[pltpu.VMEM((share * len(peers), block, mine), bf16)],
        ),
        out_shape=[jax.ShapeDtypeStruct(out, bf16)] * share,
        compiler_params=pltpu.CompilerParams(vmem_limit_bytes=24 * MIB),
        cost_estimate=pl.CostEstimate(
            flops=4 * 2 * share * len(peers) * block * block * 4 * mine,
            bytes_accessed=3 * MIB, transcendentals=0,
        ),
        name="spatial",
    )(notes, q, k, v)


def dense_kernel(axis, share, *refs):
    contexts, rest = refs[:share], refs[share:]
    x_ref, gain_ref, wo_ref, gate_ref, up_ref, down_ref = rest[:6]
    outs = rest[6:]
    member = lax.axis_index(axis) % share
    rows, mine = contexts[0].shape
    after = x_ref[...].astype(f32)
    for d in range(share):
        source = (member + share - d) % share
        after += mm(contexts[d][...], wo_ref[pl.ds(pl.multiple_of(source * mine, mine), mine), :])
    after = after.astype(bf16).astype(f32)
    x = normed(after, gain_ref[...])
    chunk = 512
    total = after
    for at in range(0, gate_ref.shape[1], chunk):
        gate = mm(x, gate_ref[:, at : at + chunk])
        up = mm(x, up_ref[:, at : at + chunk])
        hidden = (gate / (1.0 + jnp.exp(-gate)) * up).astype(bf16)
        total += mm(hidden, down_ref[at : at + chunk, :])
    block = rows // len(outs)
    for k, out_ref in enumerate(outs):
        out_ref[...] = total[k * block : (k + 1) * block].astype(bf16)


def dense(contexts, x, piece, block, gain, wo, gate, up, down, axis, share):
    rows, mine = contexts[0].shape
    width = x.shape[1]
    whole = lambda shape: pl.BlockSpec(shape, lambda i: (0,) * len(shape))
    count = rows // block
    return pl.pallas_call(
        functools.partial(dense_kernel, axis, share),
        grid=(1,),
        in_specs=[whole((rows, mine))] * share
        + [pl.BlockSpec((rows, width), lambda i: (piece, 0)), whole((1, width))]
        + [whole(w.shape) for w in (wo, gate, up, down)],
        out_specs=[whole((block, width))] * count,
        out_shape=[jax.ShapeDtypeStruct((block, width), bf16)] * count,
        compiler_params=pltpu.CompilerParams(vmem_limit_bytes=24 * MIB),
        cost_estimate=pl.CostEstimate(
            flops=2 * rows * width * (width + 3 * gate.shape[1]), bytes_accessed=8 * MIB, transcendentals=0
        ),
        name="dense",
    )(*contexts, x, gain.reshape(1, width), wo, gate, up, down)


def gather_kernel(axis, share, *refs):
    ins, out_ref, rows_ref = refs[:-2], refs[-2], refs[-1]
    steps = len(ins)
    slot = lax.axis_index(axis) // share
    block, width = ins[0].shape
    for at in range(0, width, 128):
        for r in range(steps):
            rows_ref[at // 128, pl.ds(slot ^ r, block, stride=steps), :] = ins[r][:, at : at + 128].astype(f32)
        out_ref[:, :, at : at + 128] = rows_ref[at // 128].reshape(block, steps, 128).astype(bf16)


def gather(pieces, axis, share):
    steps = len(pieces)
    block, width = pieces[0].shape
    return pl.pallas_call(
        functools.partial(gather_kernel, axis, share),
        out_shape=jax.ShapeDtypeStruct((block, steps, width), bf16),
        scratch_shapes=[pltpu.VMEM((width // 128, block * steps, 128), f32)],
        compiler_params=pltpu.CompilerParams(vmem_limit_bytes=16 * MIB),
        cost_estimate=pl.CostEstimate(flops=MIB, bytes_accessed=2 * MIB, transcendentals=0),
        name="gather",
    )(*pieces)


def per_device(
    frames, norm_time, t_wq, t_wkv, t_wo, norm_space, s_wq, s_wkv, s_wo, norm_mlp, w_gate, w_up, w_down,
    nbr_blocks, nbr_count,
):
    axis = "cell"
    block, steps, width = frames.shape
    peers_all = lax.axis_size(axis)
    share = peers_all // steps
    member = (lax.axis_index(axis) % share).astype(jnp.int32).reshape(1)

    def across(a, r):
        if r == 0:
            return a
        pairs = [(i, (i // share ^ r) * share + i % share) for i in range(peers_all)]
        return lax.ppermute(a, axis, pairs)

    def within(a, d):
        if d == 0:
            return a
        pairs = [(i, i // share * share + (i % share + d) % share) for i in range(peers_all)]
        return lax.ppermute(a, axis, pairs)

    order = list(range(steps))[::-1]
    sent = temporal(frames, norm_time, t_wq, t_wkv, t_wo, nbr_blocks, nbr_count, axis, share, peers_all)
    own = [None] * steps
    for r in order:
        own[r] = across(sent[r], r)
    pieces = [[within(a, d) for a in own] for d in range(share)]
    q, k, v, x, notes = project(pieces, norm_space, s_wq, s_wkv, axis, share, member)
    each = steps // PIECES
    landed = [None] * steps
    for piece in reversed(range(PIECES)):
        peers = tuple(range(piece * each, (piece + 1) * each))
        contexts = spatial(notes, q, k, v, block, peers, nbr_blocks.shape[1], axis, share)
        contexts = [within(c, d) for d, c in enumerate(contexts)]
        outs = dense(contexts, x, piece, block, norm_mlp, s_wo, w_gate, w_up, w_down, axis, share)
        for r, out in zip(peers, outs):
            landed[r] = across(out, r)
    return gather(landed, axis, share)


def solution(mesh):
    rows = P(("groups", "cell"))
    placed = (rows,) + (P(),) * 12 + (rows, rows)
    return jax.shard_map(per_device, mesh=mesh, in_specs=placed, out_specs=rows, check_vma=False)
```

```python
import functools
import math

import jax
import jax.numpy as jnp
from jax import lax
from jax.experimental import pallas as pl
from jax.experimental.pallas import tpu as pltpu
from jax.sharding import PartitionSpec as P

HEAD_DIM = 64
EPS = 1e-05
NEG = -1e30
PIECES = 4
NOTE = 8
AHEAD_T = 8
AHEAD_S = 3
MIB = 1 << 20


f32 = jnp.float32
bf16 = jnp.bfloat16


def normed(wide, gain):
    scale = lax.rsqrt(jnp.mean(wide * wide, axis=-1, keepdims=True) + EPS)
    return (wide * scale * gain).astype(bf16)


def mm(a, b):
    return jnp.dot(a, b, preferred_element_type=f32)


def mm_t(a, b):
    return lax.dot_general(a, b, (((1,), (1,)), ((), ())), preferred_element_type=f32)


def spread_heads(rows, group):
    if group == 1:
        return rows
    head = lax.broadcasted_iota(jnp.int32, rows.shape, 1) // HEAD_DIM
    zero = jnp.zeros_like(rows)
    return jnp.concatenate([jnp.where(head == h, rows, zero) for h in range(group)], axis=0)


def scores_of(query, key, group, mask, used):
    scores = mm_t(spread_heads(query, group), key)
    if mask is not None:
        scores = jnp.where(mask, scores, NEG)
    if used is not None:
        run = key.shape[0] // 4
        runs = [scores[:, i * run : (i + 1) * run] for i in range(4)]
        scores = jnp.concatenate(runs[:2] + [jnp.where(used > i, runs[i + 1], NEG) for i in (1, 2)], axis=1)
    return scores


def context_of(scores, value, group):
    rows, lanes = scores.shape[0] // group, value.shape[1]
    top = jnp.max(scores, axis=-1, keepdims=True)
    probs = jnp.exp(scores - top).astype(bf16)
    ones = jnp.ones(value.shape, bf16)
    both = mm(probs, jnp.concatenate([value, ones], axis=1))
    head = lax.broadcasted_iota(jnp.int32, (rows, lanes), 1) // HEAD_DIM
    context, total = both[:rows, :lanes], both[:rows, lanes:]
    for h in range(1, group):
        here = both[h * rows : (h + 1) * rows]
        context = jnp.where(head == h, here[:, :lanes], context)
        total = jnp.where(head == h, here[:, lanes:], total)
    return (context / total).astype(bf16)


def attend_all(jobs, ahead):
    ready = [score() for score, _ in jobs[:ahead]]
    for i, (_, finish) in enumerate(jobs):
        if i + ahead < len(jobs):
            ready.append(jobs[i + ahead][0]())
        finish(ready[i])
        ready[i] = None


def whole(shape):
    return pl.BlockSpec(shape, lambda *_: (0,) * len(shape))


def at(index, size):
    return pl.ds(pl.multiple_of(index * size, size), size)


ANY = pl.BlockSpec(memory_space=pl.ANY)


class Plan:
    def __init__(self, axis, devices, steps, block):
        self.axis, self.devices, self.steps, self.block = axis, devices, steps, block
        self.share = devices // steps
        self.half = steps // 2
        self.cells = block // devices
        assert devices % steps == 0 and block % devices == 0

    def place(self):
        me = lax.axis_index(self.axis)
        return me, me // self.share, me % self.share

    def across(self, a, r):
        if r == 0:
            return a
        share = self.share
        pairs = [(i, (i // share ^ r) * share + i % share) for i in range(self.devices)]
        return lax.ppermute(a, self.axis, pairs)

    def within(self, a, d):
        if d == 0:
            return a
        share = self.share
        pairs = [(i, i // share * share + (i % share + d) % share) for i in range(self.devices)]
        return lax.ppermute(a, self.axis, pairs)


def temporal_kernel(plan, nbr_ref, count_ref, frames_ref, gain_ref, wq_ref, wkv_ref, wo_ref, *rest):
    steps = plan.steps
    outs, rows_ref = rest[:-1], rest[-1]
    width = frames_ref.shape[2]
    part = plan.block // 4
    rows = part * steps
    me, slot, _ = plan.place()

    tile = math.gcd(rows, 128)
    r = lax.broadcasted_iota(jnp.int32, (2 * tile, tile), 0) % tile
    c = lax.broadcasted_iota(jnp.int32, (2 * tile, tile), 1)
    mask = (r // steps == c // steps) & (c <= r)

    @pl.loop(0, 4)
    def _(g):
        here = at(g, part)
        wide = frames_ref[here].astype(f32).reshape(rows, width)
        x = normed(wide, gain_ref[...])
        query = (mm(x, wq_ref[...]) * (HEAD_DIM**-0.5)).astype(bf16)
        pairs = mm(x, wkv_ref[...]).astype(bf16)
        parts = {}

        def job(base, lane):
            tiled = slice(base, base + tile)

            def score():
                return scores_of(query[tiled, lane : lane + 128], pairs[tiled, lane : lane + 128], 2, mask, None)

            def finish(scores):
                value = pairs[tiled, width + lane : width + lane + 128]
                parts[base, lane] = context_of(scores, value, 2)

            return score, finish

        spots = [(base, lane) for base in range(0, rows, tile) for lane in range(0, width, 128)]
        attend_all([job(*spot) for spot in spots], AHEAD_T)
        lines = [
            jnp.concatenate([parts[base, lane] for lane in range(0, width, 128)], axis=1)
            for base in range(0, rows, tile)
        ]
        mixed = wide + mm(jnp.concatenate(lines, axis=0), wo_ref[...])
        for lane in range(0, width, 128):
            rows_ref[lane // 128] = mixed[:, lane : lane + 128]
        for peer, out_ref in enumerate(outs):
            when = slot ^ peer
            for lane in range(0, width, 128):
                out_ref[here, lane : lane + 128] = rows_ref[
                    lane // 128, pl.ds(when, part, stride=steps), :
                ].astype(bf16)

    n = plan.devices
    lane = lax.broadcasted_iota(jnp.int32, (NOTE, width), 1)
    note = jnp.where(lane == 0, count_ref[0], 0)
    for i in range(nbr_ref.shape[1]):
        hop = (nbr_ref[0, i] - me + n + n // 2) % n - n // 2
        note = jnp.where(lane == i + 1, hop, note)
    note = note.astype(f32).astype(bf16)
    for out_ref in outs:
        out_ref[plan.block :, :] = note


def temporal(plan, frames, gain, wq, wkv, wo, nbr, count):
    block, steps, width = frames.shape
    messages = [block + NOTE] * steps
    smem = pl.BlockSpec(memory_space=pltpu.SMEM)
    stay = lambda a: pltpu.with_memory_space_constraint(a, pltpu.MemorySpace.HBM)
    arrays = [frames, gain.reshape(1, width), wq, wkv, wo]
    outs = pl.pallas_call(
        functools.partial(temporal_kernel, plan),
        grid=(1,),
        in_specs=[smem, smem] + [whole(a.shape) for a in arrays],
        out_specs=[whole((m, width)) for m in messages],
        scratch_shapes=[pltpu.VMEM((width // 128, block // 4 * steps, 128), f32)],
        out_shape=[jax.ShapeDtypeStruct((m, width), bf16) for m in messages],
        compiler_params=pltpu.CompilerParams(vmem_limit_bytes=24 * MIB),
        cost_estimate=pl.CostEstimate(
            flops=2 * block * steps * width * width * 4, bytes_accessed=6 * MIB, transcendentals=0
        ),
        name="temporal",
    )(nbr, count, *[stay(a) for a in arrays])
    return outs


def project_kernel(plan, labels, stacked, *refs):
    total = 1 if stacked else len(labels)
    ins, rest = refs[:total], refs[total:]
    gain_ref, wq_ref, wkv_ref, q_ref, k_ref, v_ref, x_ref = rest[:7]
    share, half, cells = plan.share, plan.half, plan.cells
    _, slot, member = plan.place()
    part = len(labels) * cells
    width = x_ref.shape[1]
    spots = x_ref.shape[0] // part
    if not stacked:
        spaced_ref = rest[-1]
        for (d, r), piece in zip(labels, ins):
            source = ((slot ^ r) & (half - 1)) * share + (member + share - d) % share
            spaced_ref[:, at(source, cells), :] = piece[: spots * cells, :].astype(f32).reshape(spots, cells, width)
            note = piece[spots * cells :, :128].astype(f32)[:1]
            rest[7][pl.ds(source, 1), :] = note.astype(jnp.int32)
    step = 4
    mine = width // share
    cols = [slice(0, mine), slice(0, mine), slice(mine, 2 * mine)]
    if wq_ref.shape[1] > mine:
        cols = [at(member, mine), at(member, mine), at(share + member, mine)]

    @pl.loop(0, spots // step)
    def _(i):
        here = at(i, step * part)
        if stacked:
            wide = ins[0][here, :].astype(f32)
        else:
            wide = spaced_ref[at(i, step)].reshape(step * part, width)
        x = normed(wide, gain_ref[...])
        q_ref[here, :] = (mm(x, wq_ref[:, cols[0]]) * (HEAD_DIM**-0.5)).astype(bf16)
        k_ref[here, :] = mm(x, wkv_ref[:, cols[1]]).astype(bf16)
        v_ref[here, :] = mm(x, wkv_ref[:, cols[2]]).astype(bf16)
        x_ref[here, :] = wide.astype(bf16)


def project(plan, pieces, gain, weights, after=()):
    labels = list(pieces)
    spots = plan.devices
    ins = [pieces[label] for label in labels]
    width = ins[0].shape[1]
    part = len(labels) * plan.cells
    mine = width // plan.share
    stacked = plan.cells % 8 != 0
    notes = []
    if stacked:
        _, slot, member = plan.place()
        source = jnp.arange(len(labels))
        d = (member + plan.share - source % plan.share) % plan.share
        r = (source // plan.share) ^ (slot & (plan.half - 1))
        pile = jnp.take(jnp.stack(ins), d * plan.half + r, axis=0)
        notes = [pile[:, spots * plan.cells, :128].astype(jnp.int32)]
        rows = pile[:, : spots * plan.cells].reshape(len(labels), spots, plan.cells, width)
        ins = [rows.transpose(1, 0, 2, 3).reshape(spots * part, width)]
    out = [((spots * part, mine), bf16)] * 3 + [((spots * part, width), bf16)]
    if not stacked:
        out.append(((len(labels), 128), jnp.int32))
    arrays = ins + [gain.reshape(1, width)] + list(weights)
    body = functools.partial(project_kernel, plan, labels, stacked)
    outs = pl.pallas_call(
        lambda *refs: body(*refs[len(after) :]),
        grid=(1,),
        in_specs=[ANY] * len(after) + [whole(a.shape) for a in arrays],
        out_specs=[whole(o) for o, _ in out],
        scratch_shapes=[] if stacked else [pltpu.VMEM((spots, part, width), f32)],
        out_shape=[jax.ShapeDtypeStruct(o, t) for o, t in out],
        compiler_params=pltpu.CompilerParams(vmem_limit_bytes=24 * MIB),
        cost_estimate=pl.CostEstimate(
            flops=2 * spots * part * width * mine * 3, bytes_accessed=4 * MIB, transcendentals=0
        ),
        name="project",
    )(*after, *arrays)
    return outs[:3], outs[3], (notes or outs[4:])


def spatial_kernel(plan, peers, notes_ref, *rest):
    share, block, n = plan.share, plan.block, plan.devices
    early, late, outs = rest[:3], rest[3:6], rest[6:]
    _, slot, member = plan.place()
    width = outs[0].shape[1]
    group = min(2, width // HEAD_DIM)
    lanes = group * HEAD_DIM
    part = block // 2

    def rows(which, b, cols):
        return [early[which][at(b, part), cols], late[which][at(b, part), cols]]

    def job(i, d, lane):
        b = (slot ^ peers[i]) * share + (member + d) % share
        note = b % (n // 2)
        blocks = [b] + [(b + notes_ref[note, 1 + k] + n) % n for k in range(3)]
        cols = slice(lane, lane + lanes)

        def score():
            key = jnp.concatenate([p for k in blocks for p in rows(1, k, cols)], axis=0)
            return scores_of(jnp.concatenate(rows(0, b, cols), axis=0), key, group, None, notes_ref[note, 0])

        def finish(scores):
            value = jnp.concatenate([p for k in blocks for p in rows(2, k, cols)], axis=0)
            outs[d][i * block : (i + 1) * block, cols] = context_of(scores, value, group)

        return score, finish

    spots = [(i, d, lane) for d in reversed(range(share)) for i in range(len(peers)) for lane in range(0, width, lanes)]
    attend_all([job(*spot) for spot in spots], AHEAD_S)


def spatial(plan, notes, sets, peers, after=()):
    block, share = plan.block, plan.share
    mine = sets[0][0].shape[1]
    out = (len(peers) * block, mine)
    arrays = [a for trio in sets for a in trio]
    body = functools.partial(spatial_kernel, plan, peers)
    return pl.pallas_call(
        lambda notes_ref, *refs: body(notes_ref, *refs[len(after) :]),
        grid_spec=pltpu.PrefetchScalarGridSpec(
            num_scalar_prefetch=1,
            grid=(1,),
            in_specs=[ANY] * len(after) + [whole(a.shape) for a in arrays],
            out_specs=[whole(out)] * share,
        ),
        out_shape=[jax.ShapeDtypeStruct(out, bf16)] * share,
        compiler_params=pltpu.CompilerParams(vmem_limit_bytes=24 * MIB),
        cost_estimate=pl.CostEstimate(
            flops=4 * 2 * share * len(peers) * block * block * 4 * mine, bytes_accessed=3 * MIB, transcendentals=0
        ),
        name="spatial",
    )(notes, *after, *arrays)


def dense_kernel(plan, peers, *refs):
    share, block = plan.share, plan.block
    contexts, rest = refs[:share], refs[share:]
    x_refs, rest = rest[:2], rest[2:]
    gain_ref, wo_ref, gate_ref, up_ref, down_ref = rest[:5]
    outs = rest[5:]
    _, slot, member = plan.place()
    mine = contexts[0].shape[1]
    part = block // 2
    pieces = []
    for r in peers:
        b = (slot ^ r) * share + member
        pieces += [x_ref[at(b, part), :].astype(f32) for x_ref in x_refs]
    after = jnp.concatenate(pieces, axis=0)
    for d in range(share):
        source = (member + share - d) % share
        after += mm(contexts[d][...], wo_ref[at(source, mine), :])
    after = after.astype(bf16).astype(f32)
    x = normed(after, gain_ref[...])
    chunk = 512
    total = after
    for start in range(0, gate_ref.shape[1], chunk):
        gate = mm(x, gate_ref[:, start : start + chunk])
        up = mm(x, up_ref[:, start : start + chunk])
        hidden = (gate / (1.0 + jnp.exp(-gate)) * up).astype(bf16)
        total += mm(hidden, down_ref[start : start + chunk, :])
    for k, out_ref in enumerate(outs):
        out_ref[...] = total[k * block : (k + 1) * block].astype(bf16)


def dense(plan, contexts, xs, peers, gain, wo, gate, up, down, after=()):
    rows = contexts[0].shape[0]
    width = xs[0].shape[1]
    arrays = list(contexts) + list(xs) + [gain.reshape(1, width), wo, gate, up, down]
    body = functools.partial(dense_kernel, plan, peers)
    out = jax.ShapeDtypeStruct((plan.block, width), bf16)
    return pl.pallas_call(
        lambda *refs: body(*refs[len(after) :]),
        grid=(1,),
        in_specs=[ANY] * len(after) + [whole(a.shape) for a in arrays],
        out_specs=[whole(out.shape)] * len(peers),
        out_shape=[out] * len(peers),
        compiler_params=pltpu.CompilerParams(vmem_limit_bytes=24 * MIB),
        cost_estimate=pl.CostEstimate(
            flops=2 * rows * width * (width + 3 * gate.shape[1]), bytes_accessed=8 * MIB, transcendentals=0
        ),
        name="dense",
    )(*after, *arrays)


def gather_kernel(plan, *refs):
    ins, out_ref, rows_ref = refs[:-2], refs[-2], refs[-1]
    steps, block = plan.steps, plan.block
    part = block // 2
    _, slot, _ = plan.place()
    for lane in range(0, out_ref.shape[2], 128):
        cols = slice(lane, lane + 128)
        for r in range(steps):
            when = slot ^ r
            early = jnp.where(when >= plan.half, part * steps, 0)
            for k in range(2):
                start = (part * steps - early if k else early) + when
                rows_ref[lane // 128, pl.ds(start, part, stride=steps), :] = ins[r][
                    k * part : (k + 1) * part, cols
                ].astype(f32)
        out_ref[:, :, cols] = rows_ref[lane // 128].reshape(block, steps, 128).astype(bf16)


def gather(plan, pieces):
    block, width = pieces[0].shape
    steps = plan.steps
    return pl.pallas_call(
        functools.partial(gather_kernel, plan),
        out_shape=jax.ShapeDtypeStruct((block, steps, width), bf16),
        scratch_shapes=[pltpu.VMEM((width // 128, block * steps, 128), f32)],
        compiler_params=pltpu.CompilerParams(vmem_limit_bytes=16 * MIB),
        cost_estimate=pl.CostEstimate(flops=MIB, bytes_accessed=2 * MIB, transcendentals=0),
        name="gather",
    )(*pieces)


def layer(
    frames, norm_time, t_wq, t_wkv, t_wo, norm_space, s_wq, s_wkv, s_wo, norm_mlp, w_gate, w_up, w_down,
    nbr_blocks, nbr_count,
):
    block, steps, width = frames.shape
    plan = Plan("cell", lax.axis_size("cell"), steps, block)
    half, share = plan.half, plan.share
    mine = width // share
    weights = [s_wq, s_wkv]
    if mine % 128:
        member = lax.axis_index("cell") % share
        take = lambda w, start: lax.dynamic_slice_in_dim(w, start * width + member * mine, mine, axis=1)
        weights = [take(s_wq, 0), jnp.concatenate([take(s_wkv, 0), take(s_wkv, 1)], axis=1)]

    def send(a, r):
        return plan.across(a, r)

    sent = temporal(plan, frames, norm_time, t_wq, t_wkv, t_wo, nbr_blocks, nbr_count)
    got = {r: send(sent[r], r) for r in reversed(range(steps))}

    def shared(peers):
        return {(d, r): plan.within(got[r], d) for d in range(share) for r in peers}

    early, x_early, (notes_early,) = project(plan, shared(range(half)), norm_space, weights)
    late, x_late, (notes_late,) = project(plan, shared(range(half, steps)), norm_space, weights, (x_early,))

    each = steps // PIECES
    peers = [tuple(range(i * each, (i + 1) * each)) for i in range(PIECES)][::-1]
    mlp = (norm_mlp, s_wo, w_gate, w_up, w_down)
    landed = [None] * steps

    def scores(i, after):
        notes = notes_late if peers[i][0] >= half else notes_early
        raw = spatial(plan, notes, (early, late), peers[i], after)
        return [plan.within(c, d) for d, c in enumerate(raw)], (raw[0],)

    def finish(i, contexts, after):
        outs = dense(plan, contexts, (x_early, x_late), peers[i], *mlp, after=after)
        for r, out in zip(peers[i], outs):
            landed[r] = send(out, r)
        return (outs[0],)

    c0, last = scores(0, ())
    last = finish(0, c0, last)
    c1, last = scores(1, last)
    c2, last = scores(2, last)
    last = finish(1, c1, last)
    c3, last = scores(3, last)
    last = finish(2, c2, last)
    finish(3, c3, last)
    return gather(plan, landed)


def solution(mesh):
    rows = P(("groups", "cell"))
    placed = (rows,) + (P(),) * 12 + (rows, rows)
    return jax.shard_map(layer, mesh=mesh, in_specs=placed, out_specs=rows, check_vma=False)
```

```python
import functools
import math

import jax
import jax.numpy as jnp
from jax import lax
from jax.experimental import pallas as pl
from jax.experimental.pallas import tpu as pltpu
from jax.sharding import PartitionSpec as P

HEAD_DIM = 64
EPS = 1e-05
NEG = -1e30
NOTE = 8
AHEAD_T = 8
AHEAD_S = 3
AHEAD_D = 2
CHUNK = 256
MIB = 1 << 20


f32 = jnp.float32
bf16 = jnp.bfloat16


def normed(wide, gain):
    scale = lax.rsqrt(jnp.mean(wide * wide, axis=-1, keepdims=True) + EPS)
    return (wide * scale * gain).astype(bf16)


def mm(a, b):
    return jnp.dot(a, b, preferred_element_type=f32)


def mm_t(a, b):
    return lax.dot_general(a, b, (((1,), (1,)), ((), ())), preferred_element_type=f32)


def spread_heads(rows, group):
    if group == 1:
        return rows
    head = lax.broadcasted_iota(jnp.int32, rows.shape, 1) // HEAD_DIM
    zero = jnp.zeros_like(rows)
    return jnp.concatenate([jnp.where(head == h, rows, zero) for h in range(group)], axis=0)


def scores_of(query, key, group, mask, used):
    scores = mm_t(spread_heads(query, group), key)
    if mask is not None:
        scores = jnp.where(mask, scores, NEG)
    if used is not None:
        run = key.shape[0] // 4
        runs = [scores[:, i * run : (i + 1) * run] for i in range(4)]
        scores = jnp.concatenate(runs[:2] + [jnp.where(used > i, runs[i + 1], NEG) for i in (1, 2)], axis=1)
    return scores


def context_of(scores, value, group):
    rows, lanes = scores.shape[0] // group, value.shape[1]
    top = jnp.max(scores, axis=-1, keepdims=True)
    probs = jnp.exp(scores - top).astype(bf16)
    ones = jnp.ones(value.shape, bf16)
    both = mm(probs, jnp.concatenate([value, ones], axis=1))
    head = lax.broadcasted_iota(jnp.int32, (rows, lanes), 1) // HEAD_DIM
    context, total = both[:rows, :lanes], both[:rows, lanes:]
    for h in range(1, group):
        here = both[h * rows : (h + 1) * rows]
        context = jnp.where(head == h, here[:, :lanes], context)
        total = jnp.where(head == h, here[:, lanes:], total)
    return (context / total).astype(bf16)


def attend_all(jobs, ahead):
    ready = [score() for score, _ in jobs[:ahead]]
    for i, (_, finish) in enumerate(jobs):
        if i + ahead < len(jobs):
            ready.append(jobs[i + ahead][0]())
        finish(ready[i])
        ready[i] = None


def whole(shape):
    return pl.BlockSpec(shape, lambda *_: (0,) * len(shape))


def at(index, size):
    return pl.ds(pl.multiple_of(index * size, size), size)


ANY = pl.BlockSpec(memory_space=pl.ANY)


class Plan:
    def __init__(self, axis, devices, steps, block):
        self.axis, self.devices, self.steps, self.block = axis, devices, steps, block
        self.share = devices // steps
        self.half = steps // 2
        self.cells = block // devices
        assert devices % steps == 0 and block % devices == 0

    def pieces(self):
        quarter = self.half // 2
        runs = [(self.half, self.half + quarter), (self.half + quarter, self.steps), (0, self.half)]
        return [tuple(range(a, b))[::-1] for a, b in runs]

    def place(self):
        me = lax.axis_index(self.axis)
        return me, me // self.share, me % self.share

    def across(self, a, r):
        if r == 0:
            return a
        share = self.share
        pairs = [(i, (i // share ^ r) * share + i % share) for i in range(self.devices)]
        return lax.ppermute(a, self.axis, pairs)

    def within(self, a, d):
        if d == 0:
            return a
        share = self.share
        pairs = [(i, i // share * share + (i % share + d) % share) for i in range(self.devices)]
        return lax.ppermute(a, self.axis, pairs)


def temporal_kernel(plan, nbr_ref, count_ref, frames_ref, gain_ref, wq_ref, wkv_ref, wo_ref, *rest):
    steps = plan.steps
    outs, rows_ref = rest[:-1], rest[-1]
    width = frames_ref.shape[2]
    part = plan.block // 4
    rows = part * steps
    me, slot, _ = plan.place()

    tile = math.gcd(rows, 128)
    r = lax.broadcasted_iota(jnp.int32, (2 * tile, tile), 0) % tile
    c = lax.broadcasted_iota(jnp.int32, (2 * tile, tile), 1)
    mask = (r // steps == c // steps) & (c <= r)

    @pl.loop(0, 4)
    def _(g):
        here = at(g, part)
        wide = frames_ref[here].astype(f32).reshape(rows, width)
        x = normed(wide, gain_ref[...])
        query = (mm(x, wq_ref[...]) * (HEAD_DIM**-0.5)).astype(bf16)
        pairs = mm(x, wkv_ref[...]).astype(bf16)
        parts = {}

        def job(base, lane):
            tiled = slice(base, base + tile)

            def score():
                return scores_of(query[tiled, lane : lane + 128], pairs[tiled, lane : lane + 128], 2, mask, None)

            def finish(scores):
                value = pairs[tiled, width + lane : width + lane + 128]
                parts[base, lane] = context_of(scores, value, 2)

            return score, finish

        spots = [(base, lane) for base in range(0, rows, tile) for lane in range(0, width, 128)]
        attend_all([job(*spot) for spot in spots], AHEAD_T)
        lines = [
            jnp.concatenate([parts[base, lane] for lane in range(0, width, 128)], axis=1)
            for base in range(0, rows, tile)
        ]
        mixed = wide + mm(jnp.concatenate(lines, axis=0), wo_ref[...])
        for lane in range(0, width, 128):
            rows_ref[lane // 128] = mixed[:, lane : lane + 128]
        for peer, out_ref in enumerate(outs):
            when = slot ^ peer
            for lane in range(0, width, 128):
                row = pl.multiple_of(lane // 128 * plan.block + g * part, 8)
                out_ref[pl.ds(row, part), :] = rows_ref[
                    lane // 128, pl.ds(when, part, stride=steps), :
                ].astype(bf16)

    n = plan.devices
    lane = lax.broadcasted_iota(jnp.int32, (NOTE, 128), 1)
    note = jnp.where(lane == 0, count_ref[0], 0)
    for i in range(nbr_ref.shape[1]):
        hop = (nbr_ref[0, i] - me + n + n // 2) % n - n // 2
        note = jnp.where(lane == i + 1, hop, note)
    note = note.astype(f32).astype(bf16)
    for out_ref in outs:
        out_ref[plan.block * width // 128 :, :] = note


def temporal(plan, frames, gain, wq, wkv, wo, nbr, count):
    block, steps, width = frames.shape
    message = (block * width // 128 + NOTE, 128)
    smem = pl.BlockSpec(memory_space=pltpu.SMEM)
    stay = lambda a: pltpu.with_memory_space_constraint(a, pltpu.MemorySpace.HBM)
    arrays = [frames, gain.reshape(1, width), wq, wkv, wo]
    outs = pl.pallas_call(
        functools.partial(temporal_kernel, plan),
        grid=(1,),
        in_specs=[smem, smem] + [whole(a.shape) for a in arrays],
        out_specs=[whole(message)] * steps,
        scratch_shapes=[pltpu.VMEM((width // 128, block // 4 * steps, 128), f32)],
        out_shape=[jax.ShapeDtypeStruct(message, bf16)] * steps,
        compiler_params=pltpu.CompilerParams(vmem_limit_bytes=24 * MIB),
        cost_estimate=pl.CostEstimate(
            flops=2 * block * steps * width * width * 4, bytes_accessed=6 * MIB, transcendentals=0
        ),
        name="temporal",
    )(nbr, count, *[stay(a) for a in arrays])
    return outs


def project_kernel(plan, labels, stacked, *refs):
    total = 1 if stacked else len(labels)
    ins, rest = refs[:total], refs[total:]
    gain_ref, wq_ref, wkv_ref, q_ref, k_ref, v_ref, x_ref = rest[:7]
    share, half, cells = plan.share, plan.half, plan.cells
    _, slot, member = plan.place()
    part = len(labels) * cells
    width = x_ref.shape[1]
    spots = x_ref.shape[0] // part
    if not stacked:
        spaced_ref = rest[-1]
        for (d, r), piece in zip(labels, ins):
            source = ((slot ^ r) & (half - 1)) * share + (member + share - d) % share
            for lane in range(0, width, 128):
                row = lane // 128 * plan.block
                spaced_ref[:, at(source, cells), lane : lane + 128] = (
                    piece[row : row + plan.block, :].astype(f32).reshape(spots, cells, 128)
                )
            note = piece[width // 128 * plan.block :, :].astype(f32)[:1]
            rest[7][pl.ds(source, 1), :] = note.astype(jnp.int32)
    step = 4
    mine = width // share
    cols = [slice(0, mine), slice(0, mine), slice(mine, 2 * mine)]
    if wq_ref.shape[1] > mine:
        cols = [at(member, mine), at(member, mine), at(share + member, mine)]

    @pl.loop(0, spots // step)
    def _(i):
        here = at(i, step * part)
        if stacked:
            wide = ins[0][here, :].astype(f32)
        else:
            wide = spaced_ref[at(i, step)].reshape(step * part, width)
        x = normed(wide, gain_ref[...])
        q_ref[here, :] = (mm(x, wq_ref[:, cols[0]]) * (HEAD_DIM**-0.5)).astype(bf16)
        k_ref[here, :] = mm(x, wkv_ref[:, cols[1]]).astype(bf16)
        v_ref[here, :] = mm(x, wkv_ref[:, cols[2]]).astype(bf16)
        x_ref[here, :] = wide.astype(bf16)


def project(plan, pieces, gain, weights, after=()):
    labels = list(pieces)
    spots = plan.devices
    ins = [pieces[label] for label in labels]
    width = weights[0].shape[0]
    part = len(labels) * plan.cells
    mine = width // plan.share
    stacked = plan.cells % 8 != 0
    notes = []
    if stacked:
        _, slot, member = plan.place()
        source = jnp.arange(len(labels))
        d = (member + plan.share - source % plan.share) % plan.share
        r = (source // plan.share) ^ (slot & (plan.half - 1))
        pile = jnp.take(jnp.stack(ins), d * plan.half + r, axis=0)
        tall = width // 128 * plan.block
        notes = [pile[:, tall].astype(jnp.int32)]
        rows = pile[:, :tall].reshape(len(labels), width // 128, spots, plan.cells, 128)
        ins = [rows.transpose(2, 0, 3, 1, 4).reshape(spots * part, width)]
    out = [((spots * part, mine), bf16)] * 3 + [((spots * part, width), bf16)]
    if not stacked:
        out.append(((len(labels), 128), jnp.int32))
    arrays = ins + [gain.reshape(1, width)] + list(weights)
    body = functools.partial(project_kernel, plan, labels, stacked)
    outs = pl.pallas_call(
        lambda *refs: body(*refs[len(after) :]),
        grid=(1,),
        in_specs=[ANY] * len(after) + [whole(a.shape) for a in arrays],
        out_specs=[whole(o) for o, _ in out],
        scratch_shapes=[] if stacked else [pltpu.VMEM((spots, part, width), f32)],
        out_shape=[jax.ShapeDtypeStruct(o, t) for o, t in out],
        compiler_params=pltpu.CompilerParams(vmem_limit_bytes=24 * MIB),
        cost_estimate=pl.CostEstimate(
            flops=2 * spots * part * width * mine * 3, bytes_accessed=4 * MIB, transcendentals=0
        ),
        name="project",
    )(*after, *arrays)
    return outs[:3], outs[3], (notes or outs[4:])


def spatial_kernel(plan, peers, notes_ref, *rest):
    share, block, n = plan.share, plan.block, plan.devices
    early, late, outs = rest[:3], rest[3:6], rest[6:]
    _, slot, member = plan.place()
    width = outs[0].shape[1]
    group = min(2, width // HEAD_DIM)
    lanes = group * HEAD_DIM
    part = block // 2

    def rows(which, b, cols):
        return [early[which][at(b, part), cols], late[which][at(b, part), cols]]

    def job(i, d, lane):
        b = (slot ^ peers[i]) * share + (member + d) % share
        note = b % (n // 2)
        blocks = [b] + [(b + notes_ref[note, 1 + k] + n) % n for k in range(3)]
        cols = slice(lane, lane + lanes)

        def score():
            key = jnp.concatenate([p for k in blocks for p in rows(1, k, cols)], axis=0)
            return scores_of(jnp.concatenate(rows(0, b, cols), axis=0), key, group, None, notes_ref[note, 0])

        def finish(scores):
            value = jnp.concatenate([p for k in blocks for p in rows(2, k, cols)], axis=0)
            outs[d][i * block : (i + 1) * block, cols] = context_of(scores, value, group)

        return score, finish

    spots = [(i, d, lane) for d in reversed(range(share)) for i in range(len(peers)) for lane in range(0, width, lanes)]
    attend_all([job(*spot) for spot in spots], AHEAD_S)


def spatial(plan, notes, sets, peers, after=()):
    block, share = plan.block, plan.share
    mine = sets[0][0].shape[1]
    out = (len(peers) * block, mine)
    arrays = [a for trio in sets for a in trio]
    body = functools.partial(spatial_kernel, plan, peers)
    return pl.pallas_call(
        lambda notes_ref, *refs: body(notes_ref, *refs[len(after) :]),
        grid_spec=pltpu.PrefetchScalarGridSpec(
            num_scalar_prefetch=1,
            grid=(1,),
            in_specs=[ANY] * len(after) + [whole(a.shape) for a in arrays],
            out_specs=[whole(out)] * share,
        ),
        out_shape=[jax.ShapeDtypeStruct(out, bf16)] * share,
        compiler_params=pltpu.CompilerParams(vmem_limit_bytes=24 * MIB),
        cost_estimate=pl.CostEstimate(
            flops=4 * 2 * share * len(peers) * block * block * 4 * mine, bytes_accessed=3 * MIB, transcendentals=0
        ),
        name="spatial",
    )(notes, *after, *arrays)


def dense_kernel(plan, peers, *refs):
    share, block = plan.share, plan.block
    contexts, rest = refs[:share], refs[share:]
    x_refs, rest = rest[:2], rest[2:]
    gain_ref, wo_ref, gate_ref, up_ref, down_ref = rest[:5]
    outs = rest[5:]
    _, slot, member = plan.place()
    mine = contexts[0].shape[1]
    part = block // 2
    pieces = []
    for r in peers:
        b = (slot ^ r) * share + member
        pieces += [x_ref[at(b, part), :].astype(f32) for x_ref in x_refs]
    after = jnp.concatenate(pieces, axis=0)
    for d in range(share):
        source = (member + share - d) % share
        after += mm(contexts[d][...], wo_ref[at(source, mine), :])
    after = after.astype(bf16).astype(f32)
    x = normed(after, gain_ref[...])
    total = after
    starts = list(range(0, gate_ref.shape[1], CHUNK))
    wide = lambda start: (mm(x, gate_ref[:, start : start + CHUNK]), mm(x, up_ref[:, start : start + CHUNK]))
    ready = [wide(start) for start in starts[:AHEAD_D]]
    for i, start in enumerate(starts):
        if i + AHEAD_D < len(starts):
            ready.append(wide(starts[i + AHEAD_D]))
        gate, up = ready[i]
        ready[i] = None
        hidden = (gate / (1.0 + jnp.exp(-gate)) * up).astype(bf16)
        total += mm(hidden, down_ref[start : start + CHUNK, :])
    for k, out_ref in enumerate(outs):
        out_ref[...] = total[k * block : (k + 1) * block].astype(bf16)


def dense(plan, contexts, xs, peers, gain, wo, gate, up, down, after=()):
    rows = contexts[0].shape[0]
    width = xs[0].shape[1]
    arrays = list(contexts) + list(xs) + [gain.reshape(1, width), wo, gate, up, down]
    body = functools.partial(dense_kernel, plan, peers)
    out = jax.ShapeDtypeStruct((plan.block, width), bf16)
    return pl.pallas_call(
        lambda *refs: body(*refs[len(after) :]),
        grid=(1,),
        in_specs=[ANY] * len(after) + [whole(a.shape) for a in arrays],
        out_specs=[whole(out.shape)] * len(peers),
        out_shape=[out] * len(peers),
        compiler_params=pltpu.CompilerParams(vmem_limit_bytes=24 * MIB),
        cost_estimate=pl.CostEstimate(
            flops=2 * rows * width * (width + 3 * gate.shape[1]), bytes_accessed=8 * MIB, transcendentals=0
        ),
        name="dense",
    )(*after, *arrays)


def gather_kernel(plan, *refs):
    ins, out_ref, rows_ref = refs[:-2], refs[-2], refs[-1]
    steps, block = plan.steps, plan.block
    part = block // 2
    _, slot, _ = plan.place()
    for lane in range(0, out_ref.shape[2], 128):
        cols = slice(lane, lane + 128)
        for r in range(steps):
            when = slot ^ r
            early = jnp.where(when >= plan.half, part * steps, 0)
            for k in range(2):
                start = (part * steps - early if k else early) + when
                rows_ref[lane // 128, pl.ds(start, part, stride=steps), :] = ins[r][
                    k * part : (k + 1) * part, cols
                ].astype(f32)
        out_ref[:, :, cols] = rows_ref[lane // 128].reshape(block, steps, 128).astype(bf16)


def gather(plan, pieces):
    block, width = pieces[0].shape
    steps = plan.steps
    return pl.pallas_call(
        functools.partial(gather_kernel, plan),
        out_shape=jax.ShapeDtypeStruct((block, steps, width), bf16),
        scratch_shapes=[pltpu.VMEM((width // 128, block * steps, 128), f32)],
        compiler_params=pltpu.CompilerParams(vmem_limit_bytes=16 * MIB),
        cost_estimate=pl.CostEstimate(flops=MIB, bytes_accessed=2 * MIB, transcendentals=0),
        name="gather",
    )(*pieces)


def layer(
    frames, norm_time, t_wq, t_wkv, t_wo, norm_space, s_wq, s_wkv, s_wo, norm_mlp, w_gate, w_up, w_down,
    nbr_blocks, nbr_count,
):
    block, steps, width = frames.shape
    plan = Plan("cell", lax.axis_size("cell"), steps, block)
    half, share = plan.half, plan.share
    mine = width // share
    weights = [s_wq, s_wkv]
    if mine % 128:
        member = lax.axis_index("cell") % share
        take = lambda w, start: lax.dynamic_slice_in_dim(w, start * width + member * mine, mine, axis=1)
        weights = [take(s_wq, 0), jnp.concatenate([take(s_wkv, 0), take(s_wkv, 1)], axis=1)]

    def send(a, r):
        return plan.across(a, r)

    sent = temporal(plan, frames, norm_time, t_wq, t_wkv, t_wo, nbr_blocks, nbr_count)
    got = {r: send(sent[r], r) for r in reversed(range(steps))}

    def shared(peers):
        return {(d, r): plan.within(got[r], d) for d in range(share) for r in peers}

    early, x_early, (notes_early,) = project(plan, shared(range(half)), norm_space, weights)
    late, x_late, (notes_late,) = project(plan, shared(range(half, steps)), norm_space, weights, (x_early,))

    peers = plan.pieces()
    mlp = (norm_mlp, s_wo, w_gate, w_up, w_down)
    landed = [None] * steps

    def scores(i, after):
        notes = notes_late if peers[i][0] >= half else notes_early
        raw = spatial(plan, notes, (early, late), peers[i], after)
        return [plan.within(c, d) for d, c in enumerate(raw)], (raw[0],)

    def finish(i, contexts, after):
        outs = dense(plan, contexts, (x_early, x_late), peers[i], *mlp, after=after)
        for r, out in zip(peers[i], outs):
            landed[r] = send(out, r)
        return (outs[0],)

    c0, last = scores(0, ())
    last = finish(0, c0, last)
    c1, last = scores(1, last)
    c2, last = scores(2, last)
    last = finish(1, c1, last)
    finish(2, c2, last)
    return gather(plan, landed)


def solution(mesh):
    rows = P(("groups", "cell"))
    placed = (rows,) + (P(),) * 12 + (rows, rows)
    return jax.shard_map(layer, mesh=mesh, in_specs=placed, out_specs=rows, check_vma=False)
```

```python
import functools
import math

import jax
import jax.numpy as jnp
from jax import lax
from jax.experimental import pallas as pl
from jax.experimental.pallas import tpu as pltpu
from jax.sharding import PartitionSpec as P

HEAD_DIM = 64
EPS = 1e-05
NEG = -1e30
NOTE = 8
AHEAD_T = 8
CHUNKS_T = 2
AHEAD_S = 3
AHEAD_D = 2
CHUNK = 256
MIB = 1 << 20


f32 = jnp.float32
bf16 = jnp.bfloat16


def normed(wide, gain):
    scale = lax.rsqrt(jnp.mean(wide * wide, axis=-1, keepdims=True) + EPS)
    return (wide * scale * gain).astype(bf16)


def mm(a, b):
    return jnp.dot(a, b, preferred_element_type=f32)


def mm_t(a, b):
    return lax.dot_general(a, b, (((1,), (1,)), ((), ())), preferred_element_type=f32)


def spread_heads(rows, group):
    if group == 1:
        return rows
    head = lax.broadcasted_iota(jnp.int32, rows.shape, 1) // HEAD_DIM
    zero = jnp.zeros_like(rows)
    return jnp.concatenate([jnp.where(head == h, rows, zero) for h in range(group)], axis=0)


def scores_of(query, key, group, mask, used):
    scores = mm_t(spread_heads(query, group), key)
    if mask is not None:
        scores = jnp.where(mask, scores, NEG)
    if used is not None:
        run = key.shape[0] // 4
        runs = [scores[:, i * run : (i + 1) * run] for i in range(4)]
        scores = jnp.concatenate(runs[:2] + [jnp.where(used > i, runs[i + 1], NEG) for i in (1, 2)], axis=1)
    return scores


def context_of(scores, value, group):
    rows, lanes = scores.shape[0] // group, value.shape[1]
    top = jnp.max(scores, axis=-1, keepdims=True)
    probs = jnp.exp(scores - top).astype(bf16)
    ones = jnp.ones(value.shape, bf16)
    both = mm(probs, jnp.concatenate([value, ones], axis=1))
    head = lax.broadcasted_iota(jnp.int32, (rows, lanes), 1) // HEAD_DIM
    context, total = both[:rows, :lanes], both[:rows, lanes:]
    for h in range(1, group):
        here = both[h * rows : (h + 1) * rows]
        context = jnp.where(head == h, here[:, :lanes], context)
        total = jnp.where(head == h, here[:, lanes:], total)
    return (context / total).astype(bf16)


def attend_all(jobs, ahead):
    ready = [score() for score, _ in jobs[:ahead]]
    for i, (_, finish) in enumerate(jobs):
        if i + ahead < len(jobs):
            ready.append(jobs[i + ahead][0]())
        finish(ready[i])
        ready[i] = None


def join(parts):
    if all(p.shape[0] % 16 == 0 for p in parts):
        return jnp.concatenate(parts, axis=0)
    return jnp.concatenate([p.astype(f32) for p in parts], axis=0).astype(parts[0].dtype)


def whole(shape):
    return pl.BlockSpec(shape, lambda *_: (0,) * len(shape))


def at(index, size):
    return pl.ds(pl.multiple_of(index * size, size), size)


ANY = pl.BlockSpec(memory_space=pl.ANY)


class Plan:
    def __init__(self, axis, devices, steps, block):
        self.axis, self.devices, self.steps, self.block = axis, devices, steps, block
        self.share = devices // steps
        self.half = steps // 2
        self.cells = block // devices
        assert devices % steps == 0 and block % devices == 0

    def pieces(self):
        quarter = self.half // 2
        runs = [(self.half, self.half + quarter), (self.half + quarter, self.steps), (0, self.half)]
        return [tuple(range(a, b))[::-1] for a, b in runs]

    def place(self):
        me = lax.axis_index(self.axis)
        return me, me // self.share, me % self.share

    def across(self, a, r):
        if r == 0:
            return a
        share = self.share
        pairs = [(i, (i // share ^ r) * share + i % share) for i in range(self.devices)]
        return lax.ppermute(a, self.axis, pairs)

    def within(self, a, d):
        if d == 0:
            return a
        share = self.share
        pairs = [(i, i // share * share + (i % share + d) % share) for i in range(self.devices)]
        return lax.ppermute(a, self.axis, pairs)


def temporal_kernel(plan, count_ref, nbr_ref, frames_ref, gain_ref, wq_ref, wkv_ref, wo_ref, *rest):
    steps = plan.steps
    outs, rows_ref = rest[:-1], rest[-1]
    width = frames_ref.shape[2]
    part = plan.block // CHUNKS_T
    rows = part * steps
    me, slot, _ = plan.place()

    tile = math.gcd(rows, 128)
    r = lax.broadcasted_iota(jnp.int32, (2 * tile, tile), 0) % tile
    c = lax.broadcasted_iota(jnp.int32, (2 * tile, tile), 1)
    mask = (r // steps == c // steps) & (c <= r)

    @pl.loop(0, CHUNKS_T)
    def _(g):
        here = at(g, part)
        wide = frames_ref[here].astype(f32).reshape(rows, width)
        x = normed(wide, gain_ref[...])
        query = (mm(x, wq_ref[...]) * (HEAD_DIM**-0.5)).astype(bf16)
        pairs = mm(x, wkv_ref[...]).astype(bf16)
        parts = {}

        def job(base, lane):
            tiled = slice(base, base + tile)

            def score():
                return scores_of(query[tiled, lane : lane + 128], pairs[tiled, lane : lane + 128], 2, mask, None)

            def finish(scores):
                value = pairs[tiled, width + lane : width + lane + 128]
                parts[base, lane] = context_of(scores, value, 2)

            return score, finish

        spots = [(base, lane) for base in range(0, rows, tile) for lane in range(0, width, 128)]
        attend_all([job(*spot) for spot in spots], AHEAD_T)
        lines = [
            jnp.concatenate([parts[base, lane] for lane in range(0, width, 128)], axis=1)
            for base in range(0, rows, tile)
        ]
        mixed = wide + mm(jnp.concatenate(lines, axis=0), wo_ref[...])
        for lane in range(0, width, 128):
            rows_ref[lane // 128] = mixed[:, lane : lane + 128]
        for peer, out_ref in enumerate(outs):
            when = slot ^ peer
            for lane in range(0, width, 128):
                row = pl.multiple_of(lane // 128 * plan.block + g * part, 8)
                out_ref[pl.ds(row, part), :] = rows_ref[
                    lane // 128, pl.ds(when, part, stride=steps), :
                ].astype(bf16)

    n = plan.devices
    lane = lax.broadcasted_iota(jnp.int32, (NOTE, 128), 1)
    note = jnp.where(lane == 0, count_ref[0], 0)
    for i in range(nbr_ref.shape[1]):
        hop = nbr_ref[:, i : i + 1] - me
        hop = jnp.where(hop > n // 2, hop - n, jnp.where(hop < -(n // 2), hop + n, hop))
        note = jnp.where(lane == i + 1, hop, note)
    note = note.astype(f32).astype(bf16)
    for out_ref in outs:
        out_ref[plan.block * width // 128 :, :] = note


def temporal(plan, frames, gain, wq, wkv, wo, nbr, count):
    block, steps, width = frames.shape
    message = (block * width // 128 + NOTE, 128)
    stay = lambda a: pltpu.with_memory_space_constraint(a, pltpu.MemorySpace.HBM)
    arrays = [nbr, frames, gain.reshape(1, width), wq, wkv, wo]
    outs = pl.pallas_call(
        functools.partial(temporal_kernel, plan),
        grid=(1,),
        in_specs=[pl.BlockSpec(memory_space=pltpu.SMEM)] + [whole(a.shape) for a in arrays],
        out_specs=[whole(message)] * steps,
        scratch_shapes=[pltpu.VMEM((width // 128, block // CHUNKS_T * steps, 128), f32)],
        out_shape=[jax.ShapeDtypeStruct(message, bf16)] * steps,
        compiler_params=pltpu.CompilerParams(vmem_limit_bytes=24 * MIB),
        cost_estimate=pl.CostEstimate(
            flops=2 * block * steps * width * width * 4, bytes_accessed=6 * MIB, transcendentals=0
        ),
        name="temporal",
    )(count, *[stay(a) for a in arrays])
    return outs


def project_kernel(plan, labels, stacked, *refs):
    total = 1 if stacked else len(labels)
    ins, rest = refs[:total], refs[total:]
    gain_ref, wq_ref, wkv_ref, q_ref, k_ref, v_ref, x_ref = rest[:7]
    share, half, cells = plan.share, plan.half, plan.cells
    _, slot, member = plan.place()
    part = len(labels) * cells
    width = x_ref.shape[1]
    spots = x_ref.shape[0] // part
    if not stacked:
        spaced_ref = rest[-1]
        for (d, r), piece in zip(labels, ins):
            source = (d - labels[0][0]) * half + ((slot ^ r) & (half - 1))
            for lane in range(0, width, 128):
                row = lane // 128 * plan.block
                spaced_ref[:, at(source, cells), lane : lane + 128] = (
                    piece[row : row + plan.block, :].astype(f32).reshape(spots, cells, 128)
                )
            note = piece[width // 128 * plan.block :, :].astype(f32)[:1]
            rest[7][pl.ds(source, 1), :] = note.astype(jnp.int32)
    step = min(spots, 256 // part)
    mine = width // share
    cols = [slice(0, mine), slice(0, mine), slice(mine, 2 * mine)]
    if wq_ref.shape[1] > mine:
        cols = [at(member, mine), at(member, mine), at(share + member, mine)]

    @pl.loop(0, spots // step)
    def _(i):
        here = at(i, step * part)
        if stacked:
            wide = ins[0][here, :].astype(f32)
        else:
            wide = spaced_ref[at(i, step)].reshape(step * part, width)
        x = normed(wide, gain_ref[...])
        q_ref[here, :] = (mm(x, wq_ref[:, cols[0]]) * (HEAD_DIM**-0.5)).astype(bf16)
        k_ref[here, :] = mm(x, wkv_ref[:, cols[1]]).astype(bf16)
        v_ref[here, :] = mm(x, wkv_ref[:, cols[2]]).astype(bf16)
        x_ref[here, :] = wide.astype(bf16)


def project(plan, pieces, gain, weights, after=()):
    labels = list(pieces)
    spots = plan.devices
    ins = [pieces[label] for label in labels]
    width = weights[0].shape[0]
    part = len(labels) * plan.cells
    mine = width // plan.share
    stacked = plan.cells % 8 != 0
    notes = []
    if stacked:
        _, slot, _ = plan.place()
        pile = jnp.take(jnp.stack(ins), jnp.arange(len(labels)) ^ (slot & (plan.half - 1)), axis=0)
        tall = width // 128 * plan.block
        notes = [pile[:, tall].astype(jnp.int32)]
        rows = pile[:, :tall].reshape(len(labels), width // 128, spots, plan.cells, 128)
        ins = [rows.transpose(2, 0, 3, 1, 4).reshape(spots * part, width)]
    out = [((spots * part, mine), bf16)] * 3 + [((spots * part, width), bf16)]
    if not stacked:
        out.append(((len(labels), 128), jnp.int32))
    arrays = ins + [gain.reshape(1, width)] + list(weights)
    body = functools.partial(project_kernel, plan, labels, stacked)
    outs = pl.pallas_call(
        lambda *refs: body(*refs[len(after) :]),
        grid=(1,),
        in_specs=[ANY] * len(after) + [whole(a.shape) for a in arrays],
        out_specs=[whole(o) for o, _ in out],
        scratch_shapes=[] if stacked else [pltpu.VMEM((spots, part, width), f32)],
        out_shape=[jax.ShapeDtypeStruct(o, t) for o, t in out],
        compiler_params=pltpu.CompilerParams(vmem_limit_bytes=24 * MIB),
        cost_estimate=pl.CostEstimate(
            flops=2 * spots * part * width * mine * 3, bytes_accessed=4 * MIB, transcendentals=0
        ),
        name="project",
    )(*after, *arrays)
    return list(outs[:3]), outs[3], (notes or outs[4:])[0]


def spatial_kernel(plan, peers, sets, noted, *refs):
    share, block, n = plan.share, plan.block, plan.devices
    notes, rest = refs[:noted], refs[noted:]
    trios, outs = [rest[3 * i : 3 * i + 3] for i in range(sets)], rest[3 * sets :]
    _, slot, member = plan.place()
    width = outs[0].shape[1]
    group = min(2, width // HEAD_DIM)
    lanes = group * HEAD_DIM

    def rows(which, b, cols):
        return [trio[which][at(b, trio[which].shape[0] // n), cols] for trio in trios]

    def job(i, d, lane):
        b = (slot ^ peers[i]) * share + (member + d) % share
        source = -d % share
        notes_ref, row = (notes[0], source) if noted == 1 or source == 0 else (notes[1], source - 1)
        note = row * plan.half + ((slot ^ peers[i]) & (plan.half - 1))
        blocks = [b] + [(b + notes_ref[note, 1 + k] + n) % n for k in range(3)]
        cols = slice(lane, lane + lanes)

        def score():
            key = join([p for k in blocks for p in rows(1, k, cols)])
            return scores_of(join(rows(0, b, cols)), key, group, None, notes_ref[note, 0])

        def finish(scores):
            value = join([p for k in blocks for p in rows(2, k, cols)])
            outs[d][i * block : (i + 1) * block, cols] = context_of(scores, value, group)

        return score, finish

    spots = [(i, d, lane) for d in reversed(range(share)) for i in range(len(peers)) for lane in range(0, width, lanes)]
    attend_all([job(*spot) for spot in spots], AHEAD_S)


def spatial(plan, notes, sets, peers, after=()):
    block, share = plan.block, plan.share
    mine = sets[0][0].shape[1]
    out = (len(peers) * block, mine)
    arrays = [a for trio in sets for a in trio]
    noted = len(notes)
    body = functools.partial(spatial_kernel, plan, peers, len(sets), noted)
    return pl.pallas_call(
        lambda *refs: body(*refs[:noted], *refs[noted + len(after) :]),
        grid_spec=pltpu.PrefetchScalarGridSpec(
            num_scalar_prefetch=noted,
            grid=(1,),
            in_specs=[ANY] * len(after) + [whole(a.shape) for a in arrays],
            out_specs=[whole(out)] * share,
        ),
        out_shape=[jax.ShapeDtypeStruct(out, bf16)] * share,
        compiler_params=pltpu.CompilerParams(vmem_limit_bytes=24 * MIB),
        cost_estimate=pl.CostEstimate(
            flops=4 * 2 * share * len(peers) * block * block * 4 * mine, bytes_accessed=3 * MIB, transcendentals=0
        ),
        name="spatial",
    )(*notes, *after, *arrays)


def dense_kernel(plan, peers, sets, *refs):
    share, block, n = plan.share, plan.block, plan.devices
    contexts, rest = refs[:share], refs[share:]
    x_refs, rest = rest[:sets], rest[sets:]
    gain_ref, wo_ref, gate_ref, up_ref, down_ref = rest[:5]
    outs = rest[5:]
    _, slot, member = plan.place()
    mine = contexts[0].shape[1]
    pieces = []
    for r in peers:
        b = (slot ^ r) * share + member
        pieces += [x_ref[at(b, x_ref.shape[0] // n), :].astype(f32) for x_ref in x_refs]
    after = jnp.concatenate(pieces, axis=0)
    part = block // 2
    run = plan.half * plan.cells
    for d in range(share):
        source = (member + share - d) % share
        more = mm(contexts[d][...], wo_ref[at(source, mine), :])
        if d:
            spots = [start + (i - d) % share * run for start in range(0, more.shape[0], part) for i in range(share)]
            more = jnp.concatenate([more[spot : spot + run] for spot in spots], axis=0)
        after += more
    after = after.astype(bf16).astype(f32)
    x = normed(after, gain_ref[...])
    total = after
    starts = list(range(0, gate_ref.shape[1], CHUNK))
    wide = lambda start: (mm(x, gate_ref[:, start : start + CHUNK]), mm(x, up_ref[:, start : start + CHUNK]))
    ready = [wide(start) for start in starts[:AHEAD_D]]
    for i, start in enumerate(starts):
        if i + AHEAD_D < len(starts):
            ready.append(wide(starts[i + AHEAD_D]))
        gate, up = ready[i]
        ready[i] = None
        hidden = (gate / (1.0 + jnp.exp(-gate)) * up).astype(bf16)
        total += mm(hidden, down_ref[start : start + CHUNK, :])
    for k, out_ref in enumerate(outs):
        out_ref[...] = total[k * block : (k + 1) * block].astype(bf16)


def dense(plan, contexts, xs, peers, place, gain, wo, gate, up, down, after=()):
    rows, mine = plan.block * len(peers), contexts[0].shape[1]
    width = xs[0].shape[1]
    arrays = list(contexts) + list(xs) + [gain.reshape(1, width), wo, gate, up, down]
    body = functools.partial(dense_kernel, plan, peers, len(xs))
    out = jax.ShapeDtypeStruct((plan.block, width), bf16)
    return pl.pallas_call(
        lambda *refs: body(*refs[len(after) :]),
        grid=(1,),
        in_specs=[ANY] * len(after)
        + [pl.BlockSpec((rows, mine), lambda i: (place, 0))] * len(contexts)
        + [whole(a.shape) for a in arrays[len(contexts) :]],
        out_specs=[whole(out.shape)] * len(peers),
        out_shape=[out] * len(peers),
        compiler_params=pltpu.CompilerParams(vmem_limit_bytes=24 * MIB),
        cost_estimate=pl.CostEstimate(
            flops=2 * rows * width * (width + 3 * gate.shape[1]), bytes_accessed=8 * MIB, transcendentals=0
        ),
        name="dense",
    )(*after, *arrays)


def gather_kernel(plan, *refs):
    ins, out_ref, rows_ref = refs[:-2], refs[-2], refs[-1]
    steps, block = plan.steps, plan.block
    share, half, cells = plan.share, plan.half, plan.cells
    part = block // 2
    _, slot, member = plan.place()
    for lane in range(0, out_ref.shape[2], 128):
        cols = slice(lane, lane + 128)
        for r in range(steps):
            when = slot ^ r
            early = jnp.where(when >= half, half, 0)
            for first, wide in ((early, ins[r][:part, cols]), (half - early, ins[r][part:, cols])):
                wide = wide.astype(f32)
                for i in range(share):
                    for c in range(half):
                        cell = ((first + c) * share + (member + share - i) % share) * cells
                        row = (i * half + c) * cells
                        rows_ref[lane // 128, pl.ds(cell * steps + when, cells, stride=steps), :] = wide[
                            row : row + cells
                        ]
        out_ref[:, :, cols] = rows_ref[lane // 128].reshape(block, steps, 128).astype(bf16)


def gather(plan, pieces):
    block, width = pieces[0].shape
    steps = plan.steps
    return pl.pallas_call(
        functools.partial(gather_kernel, plan),
        out_shape=jax.ShapeDtypeStruct((block, steps, width), bf16),
        scratch_shapes=[pltpu.VMEM((width // 128, block * steps, 128), f32)],
        compiler_params=pltpu.CompilerParams(vmem_limit_bytes=16 * MIB),
        cost_estimate=pl.CostEstimate(flops=MIB, bytes_accessed=2 * MIB, transcendentals=0),
        name="gather",
    )(*pieces)


def layer(
    frames, norm_time, t_wq, t_wkv, t_wo, norm_space, s_wq, s_wkv, s_wo, norm_mlp, w_gate, w_up, w_down,
    nbr_blocks, nbr_count,
):
    block, steps, width = frames.shape
    plan = Plan("cell", lax.axis_size("cell"), steps, block)
    half, share = plan.half, plan.share
    mine = width // share
    weights = [s_wq, s_wkv]
    if mine % 128:
        member = lax.axis_index("cell") % share
        take = lambda w, start: lax.dynamic_slice_in_dim(w, start * width + member * mine, mine, axis=1)
        weights = [take(s_wq, 0), jnp.concatenate([take(s_wkv, 0), take(s_wkv, 1)], axis=1)]

    def send(a, r):
        return plan.across(a, r)

    sent = temporal(plan, frames, norm_time, t_wq, t_wkv, t_wo, nbr_blocks, nbr_count)
    got = {r: send(sent[r], r) for r in reversed(range(steps))}

    def shared(peers):
        return {(d, r): plan.within(got[r], d) for d in range(share) for r in peers}

    near = shared(range(half))
    early, x_early, notes_early = project(plan, near, norm_space, weights)
    late = shared(range(half, steps))
    own, x_own, notes_own = project(plan, {k: a for k, a in late.items() if k[0] == 0}, norm_space, weights, (x_early,))
    others, x_others, notes_others = project(
        plan, {k: a for k, a in late.items() if k[0]}, norm_space, weights, (x_own,)
    )

    peers = plan.pieces()
    mlp = (norm_mlp, s_wo, w_gate, w_up, w_down)
    landed = [None] * steps

    def scores(i, after):
        notes = (notes_own, notes_others) if peers[i][0] >= half else (notes_early,)
        raw = spatial(plan, notes, (early, own, others), peers[i], after)
        return [plan.within(c, d) for d, c in enumerate(raw)], (raw[0],)

    def finish(i, contexts, after, start=0, stop=2):
        each = half // 2
        for place in range(start, stop):
            served = peers[i][place * each : (place + 1) * each]
            outs = dense(plan, contexts, (x_early, x_own, x_others), served, place, *mlp, after=after)
            after = (outs[0],)
            for r, out in zip(served, outs):
                landed[r] = send(out, r)
        return after

    c0, last = scores(0, ())
    c1, last = scores(1, last)
    last = finish(0, c0, last, 0, 1)
    c2, last = scores(2, last)
    last = finish(1, c1, last, 0, 1)
    last = finish(2, c2, last, 0, 1)
    finish(2, c2, last, 1, 2)
    return gather(plan, landed)


def solution(mesh):
    rows = P(("groups", "cell"))
    placed = (rows,) + (P(),) * 12 + (rows, rows)
    return jax.shard_map(layer, mesh=mesh, in_specs=placed, out_specs=rows, check_vma=False)
```
